32 devices in a mesh: groups: 2 (over x), kvseq: 8 (over z, y), tensor: 2 (over core).
Axes of the slice: x: 2, y: 2, z: 4, core: 2. Of those that a mesh axis runs over, the one named last changes fastest.
Arguments:
- hidden: bfloat16 [16, 8192], P('groups', 'kvseq'), parts along dimension 0, may hold values from -30 to 30
- lengths: int32 [16], P('groups'), parts along dimension 0, may hold values from 128 to 2048, as said below
- key_cache: bfloat16 [16, 2048, 1024], P('groups', 'kvseq', 'tensor'), parts along dimension 0, may hold values from -400 to 400
- value_cache: bfloat16 [16, 2048, 1024], P('groups', 'kvseq', 'tensor'), parts along dimension 0, may hold values from -60 to 60
- gain_in: float32 [8192], P('kvseq'), may hold values from 0.1 to 1.9
- w_query: bfloat16 [8192, 8192], P('kvseq', 'tensor'), may hold values from -0.0625 to 0.0625
- w_key: bfloat16 [8192, 1024], P('kvseq', 'tensor'), may hold values from -0.0625 to 0.0625
- w_value: bfloat16 [8192, 1024], P('kvseq', 'tensor'), may hold values from -0.0625 to 0.0625
- w_output: bfloat16 [8192, 8192], P('tensor', 'kvseq'), may hold values from -0.0625 to 0.0625
- gain_post: float32 [8192], P('kvseq'), may hold values from 0.1 to 1.9
- w_gate: bfloat16 [8192, 15360], P('kvseq', 'tensor'), may hold values from -0.0625 to 0.0625
- w_up: bfloat16 [8192, 15360], P('kvseq', 'tensor'), may hold values from -0.0625 to 0.0625
- w_down: bfloat16 [15360, 8192], P('tensor', 'kvseq'), may hold values from -0.046875 to 0.046875
Outputs:
- output: bfloat16 [16, 8192], P('groups', 'kvseq'), parts along dimension 0
- new_keys: bfloat16 [16, 1024], P('groups', 'tensor'), parts along dimension 0
- new_values: bfloat16 [16, 1024], P('groups', 'tensor'), parts along dimension 0
The draws below stay inside these ranges and needn't reach their ends.
There are 2 independent parts, one for each index of `groups`. The reference program is written for one: setup_inputs(seed, part) draws one part's arguments, and reference() takes and returns one part's arrays. A program takes and returns all parts, laid end to end along the dimension named above; an argument that names none is the same for every part. Nothing has to cross between parts.
Inputs may be any that keep to these rules, and one draw needn't show every extreme that they name: `lengths`: multiples of 128; some sequence holds exactly 2048.
All inputs are finite; a program needn't handle non-finite values.
Results may differ from the reference program's by a relative error of at most 0.024.
Values may be sent and summed in bfloat16 or wider, within the bound.
No kernel may reach another device: no remote copies, remote signals or barrier semaphores. Data moves between devices by JAX's collectives and lax.ppermute only.
A program may use at most 128 MiB of HBM per device.

```python
import jax
import jax.numpy as jnp
from jax import lax

D = 8192
H = 64
KVH = 8
HD = 128
FF = 15360
SEQS = 8
PAGE = 128
LENGTH = 2048


def draw_hidden(key, part):
    ramp = jnp.exp(jnp.linspace(0.0, jnp.log(3.0), D)).astype(jnp.float32)
    rough = jax.random.uniform(jax.random.fold_in(key, 11), (D,), jnp.float32, 0.5, 1.5)
    base = jnp.clip(jax.random.normal(jax.random.fold_in(key, 12), (SEQS, D), jnp.float32), -6.0, 6.0)
    return (base * ramp * rough).astype(jnp.bfloat16)


def draw_lengths(key, part):
    pages = jax.random.randint(jax.random.fold_in(key, 21), (SEQS,), 1, LENGTH // PAGE + 1) * PAGE
    chosen = jax.random.randint(jax.random.fold_in(key, 22), (), 0, SEQS)
    return pages.at[chosen].set(LENGTH).astype(jnp.int32)


def draw_key_cache(key, part):
    base = jnp.clip(jax.random.normal(jax.random.fold_in(key, 31), (SEQS, LENGTH, KVH * HD), jnp.float32), -6.0, 6.0)
    return base.astype(jnp.bfloat16)


def draw_value_cache(key, part):
    place = jnp.arange(LENGTH, dtype=jnp.float32) / LENGTH
    magnitude = jax.random.uniform(jax.random.fold_in(key, 41), (KVH * HD,), jnp.float32, 0.5, 1.5)
    sign = jnp.where(jax.random.bernoulli(jax.random.fold_in(key, 42), 0.5, (KVH * HD,)), 1.0, -1.0)
    common = 1.5 * magnitude * sign
    ramp = jnp.exp(place * jnp.log(4.0))
    rough = jnp.clip(jax.random.normal(jax.random.fold_in(key, 43), (SEQS, LENGTH, KVH * HD), jnp.float32), -3.0, 3.0)
    values = (rough + common[None, None, :]) * ramp[None, :, None]
    return values.astype(jnp.bfloat16)


def shard_levels(rng, extent, shards, least, high):
    level = 1.0
    for dim, parts in shards:
        draws = jax.random.uniform(jax.random.fold_in(jax.random.fold_in(rng, 6), dim), (parts,), jnp.float32, least / len(shards), high / len(shards))
        level = level * jnp.repeat(jnp.exp(draws), extent[dim] // parts).reshape((-1,) + (1,) * (len(extent) - 1 - dim))
    return level


def bell_draw(rng, shape, spread, limit, split=(), kind=jnp.bfloat16):
    drawn = spread * jax.random.normal(rng, shape, jnp.float32)
    if split:
        drawn = drawn * shard_levels(rng, shape, split, -0.22, 0.18)
    return jnp.clip(drawn, -limit, limit).astype(kind)


def setup_inputs(seed: int = 0, part: int = 0) -> dict:
    key_list = jax.random.split(jax.random.key(seed), 14)
    part_splits = jax.random.split(jax.random.fold_in(key_list[13], part), 14)
    hidden = draw_hidden(jax.random.fold_in(jax.random.fold_in(key_list[13], part), 71), part)
    lengths = draw_lengths(jax.random.fold_in(jax.random.fold_in(key_list[13], part), 71), part)
    key_cache = draw_key_cache(jax.random.fold_in(jax.random.fold_in(key_list[13], part), 71), part)
    value_cache = draw_value_cache(jax.random.fold_in(jax.random.fold_in(key_list[13], part), 71), part)
    gain_in = jnp.clip(1.0 + 0.18 * jax.random.normal(key_list[4], (D,), jnp.float32), 0.1, 1.9)
    w_query = bell_draw(key_list[5], (D, H * HD), D ** -0.5, 0.0625, ((0, 8), (1, 2)))
    w_key = bell_draw(key_list[6], (D, KVH * HD), D ** -0.5, 0.0625, ((0, 8), (1, 2)))
    w_value = bell_draw(key_list[7], (D, KVH * HD), D ** -0.5, 0.0625, ((0, 8), (1, 2)))
    w_output = bell_draw(key_list[8], (H * HD, D), (H * HD) ** -0.5, 0.0625, ((0, 2), (1, 8)))
    gain_post = jnp.clip(1.0 + 0.18 * jax.random.normal(key_list[9], (D,), jnp.float32), 0.1, 1.9)
    w_gate = bell_draw(key_list[10], (D, FF), D ** -0.5, 0.0625, ((0, 8), (1, 2)))
    w_up = bell_draw(key_list[11], (D, FF), D ** -0.5, 0.0625, ((0, 8), (1, 2)))
    w_down = bell_draw(key_list[12], (FF, D), FF ** -0.5, 0.046875, ((0, 2), (1, 8)))
    return dict(hidden=hidden, lengths=lengths, key_cache=key_cache, value_cache=value_cache, gain_in=gain_in, w_query=w_query, w_key=w_key, w_value=w_value, w_output=w_output, gain_post=gain_post, w_gate=w_gate, w_up=w_up, w_down=w_down)


epsilon = 1e-06
rope_base = 1000000.0

def rotate(values, position):
    half_dim = values.shape[-1] // 2
    frequency = rope_base ** (-jnp.arange(half_dim, dtype=jnp.float32) * 2.0 / values.shape[-1])
    angles = position[:, None, None] * frequency
    cosine = jnp.cos(angles)
    sine = jnp.sin(angles)
    lower = values[..., :half_dim]
    upper = values[..., half_dim:]
    return jnp.concatenate([lower * cosine - upper * sine, upper * cosine + lower * sine], axis=-1)

def rms_norm(stream, gain):
    scale = lax.rsqrt(lax.optimization_barrier(jnp.mean(stream * stream, axis=1, keepdims=True)) + epsilon)
    return (stream * scale * gain).astype(jnp.bfloat16)

def reference(hidden, lengths, key_cache, value_cache, gain_in, w_query, w_key, w_value, w_output, gain_post, w_gate, w_up, w_down):
    stream = hidden.astype(jnp.float32)
    normed = rms_norm(stream, gain_in)
    query = jnp.dot(normed, w_query, preferred_element_type=jnp.float32)
    key = jnp.dot(normed, w_key, preferred_element_type=jnp.float32)
    value = jnp.dot(normed, w_value, preferred_element_type=jnp.float32)
    position = lengths.astype(jnp.float32)
    query = rotate(query.reshape(SEQS, H, HD), position)
    new_keys = rotate(key.reshape(SEQS, KVH, HD), position).astype(jnp.bfloat16)
    new_values = value.reshape(SEQS, KVH, HD).astype(jnp.bfloat16)
    grouped = query.astype(jnp.bfloat16).reshape(SEQS, KVH, H // KVH, HD).astype(jnp.float32)
    cached_keys = key_cache.reshape(SEQS, LENGTH, KVH, HD).astype(jnp.float32)
    cached_values = value_cache.reshape(SEQS, LENGTH, KVH, HD).astype(jnp.float32)
    factor = float(HD) ** (-0.5)
    scores = jnp.einsum('skgd,slkd->skgl', grouped, cached_keys) * factor
    valid = (jnp.arange(LENGTH, dtype=jnp.int32)[None, :] < lengths[:, None])[:, None, None, :]
    masked = jnp.where(valid, scores, -1e+30)
    own = jnp.einsum('skgd,skd->skg', grouped, new_keys.astype(jnp.float32)) * factor
    top = jnp.maximum(lax.optimization_barrier(jnp.max(masked, axis=-1)), own)
    weights = jnp.where(valid, jnp.exp(masked - top[..., None]), 0.0)
    own_weight = jnp.exp(own - top)
    total = lax.optimization_barrier(jnp.sum(weights, axis=-1)) + own_weight
    mixed = jnp.einsum('skgl,slkd->skgd', weights.astype(jnp.bfloat16).astype(jnp.float32), cached_values)
    mixed = mixed + own_weight[..., None] * new_values.astype(jnp.float32)[:, :, None, :]
    attended = (mixed / total[..., None]).astype(jnp.bfloat16).reshape(SEQS, H * HD)
    residual = stream + jnp.dot(attended, w_output, preferred_element_type=jnp.float32)
    normed_post = rms_norm(residual, gain_post)
    gate = jnp.dot(normed_post, w_gate, preferred_element_type=jnp.float32)
    upward = jnp.dot(normed_post, w_up, preferred_element_type=jnp.float32)
    inner = (jax.nn.silu(gate) * upward).astype(jnp.bfloat16)
    output = (residual + jnp.dot(inner, w_down, preferred_element_type=jnp.float32)).astype(jnp.bfloat16)
    return (output, new_keys.reshape(SEQS, KVH * HD), new_values.reshape(SEQS, KVH * HD))
```

```python
import jax
import jax.numpy as jnp
from jax import lax
from jax.sharding import PartitionSpec as P

D = 8192
HD = 128


epsilon = 1e-06
rope_base = 1000000.0


def rounded(x):
    return lax.reduce_precision(x, exponent_bits=8, mantissa_bits=7)


def split_high_low(x):
    high = rounded(x)
    return high, rounded(x - high)


def exchange(x, axis, bit):
    count = lax.axis_size(axis)
    return lax.ppermute(x, axis, [(i, i ^ bit) for i in range(count)])


def bits_of(axis):
    count = lax.axis_size(axis)
    return [1 << i for i in range(count.bit_length() - 1)]


def sum_by_doubling(x, axis, bits):
    for bit in bits:
        sent = x.astype(jnp.bfloat16)
        got = exchange(sent, axis, bit)
        x = sent.astype(jnp.float32) + got.astype(jnp.float32)
    return x


def sum_with_scalars(x, scalars, axis, bits):
    rows, width = x.shape
    for bit in bits:
        high, low = split_high_low(scalars)
        packed = jnp.concatenate(
            [
                x.astype(jnp.bfloat16),
                jnp.broadcast_to(high[:, None], (rows, 128)).astype(jnp.bfloat16),
                jnp.broadcast_to(low[:, None], (rows, 128)).astype(jnp.bfloat16),
            ],
            axis=1,
        )
        got = exchange(packed, axis, bit)
        both = packed.astype(jnp.float32) + got.astype(jnp.float32)
        x = both[:, :width]
        scalars = both[:, width] + both[:, width + 128]
    return x, scalars


def rotate(values, position):
    half_dim = values.shape[-1] // 2
    frequency = rope_base ** (-jnp.arange(half_dim, dtype=jnp.float32) * 2.0 / values.shape[-1])
    angles = position[:, None, None] * frequency
    cosine = jnp.cos(angles)
    sine = jnp.sin(angles)
    lower = values[..., :half_dim]
    upper = values[..., half_dim:]
    return jnp.concatenate([lower * cosine - upper * sine, upper * cosine + lower * sine], axis=-1)


def combine_parts(earlier, later_part):
    top = jnp.maximum(earlier[0], later_part[0])
    scale_one = jnp.exp(earlier[0] - top)
    scale_two = jnp.exp(later_part[0] - top)
    total = earlier[1] * scale_one + later_part[1] * scale_two
    mixed = earlier[2] * scale_one[..., None] + later_part[2] * scale_two[..., None]
    return (top, total, mixed)


def per_device(
    hidden,
    lengths,
    key_cache,
    value_cache,
    gain_in,
    w_query,
    w_key,
    w_value,
    w_output,
    gain_post,
    w_gate,
    w_up,
    w_down,
):
    stream = hidden.astype(jnp.float32)
    bits = bits_of("kvseq")
    squares = jnp.sum(stream * stream, axis=1)
    weighted = (stream * gain_in).astype(jnp.bfloat16)
    parts = [
        jnp.dot(weighted, w, preferred_element_type=jnp.float32) for w in (w_query, w_key, w_value)
    ]
    joined, squares = sum_with_scalars(jnp.concatenate(parts, axis=1), squares, "kvseq", bits)
    joined = joined * lax.rsqrt(squares / D + epsilon)[:, None]
    q_width, k_width = w_query.shape[1], w_key.shape[1]
    query = joined[:, :q_width]
    key = joined[:, q_width : q_width + k_width]
    value = joined[:, q_width + k_width :]
    seq_count = hidden.shape[0]
    query_heads = w_query.shape[1] // HD
    kv_heads = w_key.shape[1] // HD
    per_group = query_heads // kv_heads
    position = lengths.astype(jnp.float32)
    query = rotate(query.reshape(seq_count, query_heads, HD), position)
    new_keys = rotate(key.reshape(seq_count, kv_heads, HD), position).astype(jnp.bfloat16)
    new_values = value.reshape(seq_count, kv_heads, HD).astype(jnp.bfloat16)
    grouped = query.astype(jnp.bfloat16).reshape(seq_count, kv_heads, per_group, HD)
    local_len = key_cache.shape[1]
    cached_keys = key_cache.reshape(seq_count, local_len, kv_heads, HD)
    cached_values = value_cache.reshape(seq_count, local_len, kv_heads, HD)
    factor = float(HD) ** (-0.5)
    scores = (
        jnp.einsum("skgd,slkd->skgl", grouped, cached_keys, preferred_element_type=jnp.float32)
        * factor
    )
    offsets = lax.axis_index("kvseq") * local_len + jnp.arange(local_len, dtype=jnp.int32)
    valid = (offsets[None, :] < lengths[:, None])[:, None, None, :]
    masked = jnp.where(valid, scores, -1e30)
    local_top = sum(split_high_low(jnp.max(masked, axis=-1)))
    weights = jnp.where(valid, jnp.exp(masked - local_top[..., None]), 0.0)
    local_total = jnp.sum(weights, axis=-1)
    local_mixed = jnp.einsum(
        "skgl,slkd->skgd",
        weights.astype(jnp.bfloat16),
        cached_values,
        preferred_element_type=jnp.float32,
    )
    top, total, mixed = local_top, local_total, local_mixed
    for bit in bits:
        top_parts = split_high_low(top)
        total_parts = split_high_low(total)
        stats = jnp.concatenate(
            [a.reshape(seq_count, query_heads) for a in top_parts + total_parts], axis=1
        ).astype(jnp.bfloat16)
        packed = jnp.concatenate(
            [mixed.reshape(seq_count, query_heads * HD).astype(jnp.bfloat16), stats], axis=1
        )
        got = exchange(packed, "kvseq", bit)

        def unpack(array):
            array = array.astype(jnp.float32)
            part = array[:, query_heads * HD :].reshape(seq_count, 4, kv_heads, per_group)
            return (
                part[:, 0] + part[:, 1],
                part[:, 2] + part[:, 3],
                array[:, : query_heads * HD].reshape(seq_count, kv_heads, per_group, HD),
            )

        top, total, mixed = combine_parts(unpack(packed), unpack(got))
    own = (
        jnp.einsum("skgd,skd->skg", grouped, new_keys, preferred_element_type=jnp.float32) * factor
    )
    final_top = jnp.maximum(top, own)
    old_scale = jnp.exp(top - final_top)
    own_weight = jnp.exp(own - final_top)
    total = total * old_scale + own_weight
    mixed = (
        mixed * old_scale[..., None]
        + own_weight[..., None] * new_values.astype(jnp.float32)[:, :, None, :]
    )
    attended = (mixed / total[..., None]).astype(jnp.bfloat16).reshape(seq_count, query_heads * HD)
    projected = jnp.dot(attended, w_output, preferred_element_type=jnp.float32)
    residual = stream + (projected + lax.ppermute(projected, "tensor", [(0, 1), (1, 0)]))
    squares_post = jnp.sum(residual * residual, axis=1)
    weighted_post = (residual * gain_post).astype(jnp.bfloat16)
    gate_part = jnp.dot(weighted_post, w_gate, preferred_element_type=jnp.float32)
    upward_part = jnp.dot(weighted_post, w_up, preferred_element_type=jnp.float32)
    half = w_gate.shape[1] // 2
    upper_half = (lax.axis_index("kvseq") & 1) == 1
    lower = jnp.concatenate([gate_part[:, :half], upward_part[:, :half]], axis=1)
    upper = jnp.concatenate([gate_part[:, half:], upward_part[:, half:]], axis=1)
    high, low = split_high_low(squares_post)
    scalars = jnp.concatenate(
        [jnp.broadcast_to(a[:, None], (seq_count, 128)) for a in (high, low)], axis=1
    )
    lower = jnp.concatenate([lower, scalars], axis=1).astype(jnp.bfloat16)
    upper = jnp.concatenate([upper, scalars], axis=1).astype(jnp.bfloat16)
    sent = jnp.where(upper_half, lower, upper)
    kept = jnp.where(upper_half, upper, lower)
    got = exchange(sent, "kvseq", 1)
    both = kept.astype(jnp.float32) + got.astype(jnp.float32)
    both, squares_post = sum_with_scalars(
        both[:, : 2 * half], both[:, 2 * half] + both[:, 2 * half + 128], "kvseq", bits[1:]
    )
    both = both * lax.rsqrt(squares_post / D + epsilon)[:, None]
    gate, upward = both[:, :half], both[:, half:]
    mine = (jax.nn.silu(gate) * upward).astype(jnp.bfloat16)
    other = exchange(mine, "kvseq", 1)
    inner = jnp.where(
        upper_half,
        jnp.concatenate([other, mine], axis=1),
        jnp.concatenate([mine, other], axis=1),
    )
    down_part = jnp.dot(inner, w_down, preferred_element_type=jnp.float32)
    down = down_part + lax.ppermute(down_part, "tensor", [(0, 1), (1, 0)])
    output = (residual + down).astype(jnp.bfloat16)
    return (
        output,
        new_keys.reshape(seq_count, kv_heads * HD),
        new_values.reshape(seq_count, kv_heads * HD),
    )


def solution(mesh):
    placed = (
        P("groups", "kvseq"),
        P("groups"),
        P("groups", "kvseq", "tensor"),
        P("groups", "kvseq", "tensor"),
        P("kvseq"),
        P("kvseq", "tensor"),
        P("kvseq", "tensor"),
        P("kvseq", "tensor"),
        P("tensor", "kvseq"),
        P("kvseq"),
        P("kvseq", "tensor"),
        P("kvseq", "tensor"),
        P("tensor", "kvseq"),
    )
    return jax.shard_map(
        per_device,
        mesh=mesh,
        in_specs=placed,
        out_specs=(P("groups", "kvseq"), P("groups", "tensor"), P("groups", "tensor")),
        check_vma=False,
    )
```

```python
import jax
import jax.numpy as jnp
from jax import lax
from jax.experimental import pallas as pl
from jax.experimental.pallas import tpu as pltpu
from jax.sharding import PartitionSpec as P

D = 8192
HD = 128


epsilon = 1e-06
rope_base = 1000000.0


def high_low(x):
    high = x.astype(jnp.bfloat16).astype(jnp.float32)
    low = (x - high).astype(jnp.bfloat16).astype(jnp.float32)
    return high, low


def split_high_low(x):
    high = lax.reduce_precision(x, exponent_bits=8, mantissa_bits=7)
    return high, lax.reduce_precision(x - high, exponent_bits=8, mantissa_bits=7)


def exchange(x, axis, bit):
    count = lax.axis_size(axis)
    return lax.ppermute(x, axis, [(i, i ^ bit) for i in range(count)])


def bits_of(axis):
    count = lax.axis_size(axis)
    return [1 << i for i in range(count.bit_length() - 1)]


WAIT_FLOPS = 1500000000


def local_call(kernel, outs, *args, flops=0, name=None):
    single = not isinstance(outs, (list, tuple))
    return pl.pallas_call(
        kernel,
        out_shape=outs,
        in_specs=[pl.BlockSpec(memory_space=pltpu.VMEM) for _ in args],
        out_specs=(
            pl.BlockSpec(memory_space=pltpu.VMEM)
            if single
            else [pl.BlockSpec(memory_space=pltpu.VMEM) for _ in outs]
        ),
        compiler_params=pltpu.CompilerParams(vmem_limit_bytes=4 << 20),
        cost_estimate=pl.CostEstimate(flops=flops, bytes_accessed=0, transcendentals=0),
        name=name,
    )(*args)


def like(*shape, dtype=jnp.bfloat16):
    return jax.ShapeDtypeStruct(shape, dtype)


def sums(own_ref, got_ref):
    width = own_ref.shape[1] - 256
    own = own_ref[...].astype(jnp.float32)
    both = own + got_ref[...].astype(jnp.float32)
    scalar = both[:, width : width + 128] + both[:, width + 128 :]
    return both[:, :width], scalar


def sum_kernel(own_ref, got_ref, out_ref):
    width = own_ref.shape[1] - 256
    both, scalar = sums(own_ref, got_ref)
    high, low = high_low(scalar)
    out_ref[:, :width] = both.astype(out_ref.dtype)
    out_ref[:, width : width + 128] = high.astype(out_ref.dtype)
    out_ref[:, width + 128 :] = low.astype(out_ref.dtype)


def turned(x, cosine, sine):
    return x * cosine + pltpu.roll(x, HD // 2, 1) * sine


def query_kernel(own_ref, got_ref, angle_ref, query_ref, key_ref, value_ref, rows_ref):
    both, scalar = sums(own_ref, got_ref)
    scale = lax.rsqrt(scalar / D + epsilon)
    cosine, sine = angle_ref[:, :HD], angle_ref[:, HD:]
    q_width, k_width = query_ref.shape[1], key_ref.shape[1]
    for h in range(q_width // HD):
        part = both[:, h * HD : (h + 1) * HD] * scale
        part = turned(part, cosine, sine).astype(query_ref.dtype)
        query_ref[:, h * HD : (h + 1) * HD] = part
        rows_ref[:, h, :] = part.astype(rows_ref.dtype)
    for h in range(k_width // HD):
        at = q_width + h * HD
        part = both[:, at : at + HD] * scale
        key_ref[:, h * HD : (h + 1) * HD] = turned(part, cosine, sine).astype(key_ref.dtype)
        at = at + k_width
        value_ref[:, h * HD : (h + 1) * HD] = (both[:, at : at + HD] * scale).astype(value_ref.dtype)


def shifted(x, lanes):
    size = x.shape[1]
    return pltpu.roll(x, lanes % size, 1)


def joined_parts(own_ref, got_ref, heads):
    width = heads * HD
    stats_own = own_ref[:, width:].astype(jnp.float32)
    stats_got = got_ref[:, width:].astype(jnp.float32)

    def tops(x):
        return x + shifted(x, -heads)

    def totals(x):
        return shifted(x, -2 * heads) + shifted(x, -3 * heads)

    top_own, top_got = tops(stats_own), tops(stats_got)
    top = jnp.maximum(top_own, top_got)
    lane = lax.broadcasted_iota(jnp.int32, top.shape, 1)
    used = lane < heads
    scale_own = jnp.exp(jnp.where(used, top_own - top, 0.0))
    scale_got = jnp.exp(jnp.where(used, top_got - top, 0.0))
    total = totals(stats_own) * scale_own + totals(stats_got) * scale_got

    def mixed(h):
        at = slice(h * HD, (h + 1) * HD)
        return own_ref[:, at].astype(jnp.float32) * scale_own[:, h : h + 1] + got_ref[:, at].astype(
            jnp.float32
        ) * scale_got[:, h : h + 1]

    return top, total, mixed, lane


def packed_stats(top, total, lane, heads):
    top_high, top_low = high_low(top)
    total_high, total_low = high_low(total)
    return jnp.where(
        lane < heads,
        top_high,
        jnp.where(
            lane < 2 * heads,
            shifted(top_low, heads),
            jnp.where(lane < 3 * heads, shifted(total_high, 2 * heads), shifted(total_low, 3 * heads)),
        ),
    )


def join_kernel(own_ref, got_ref, out_ref):
    heads = (own_ref.shape[1] - 128) // HD
    top, total, mixed, lane = joined_parts(own_ref, got_ref, heads)
    for h in range(heads):
        out_ref[:, h * HD : (h + 1) * HD] = mixed(h).astype(out_ref.dtype)
    out_ref[:, heads * HD :] = packed_stats(top, total, lane, heads).astype(out_ref.dtype)


def attended_kernel(own_ref, got_ref, query_ref, key_ref, value_ref, out_ref):
    heads = query_ref.shape[1] // HD
    group = query_ref.shape[1] // key_ref.shape[1]
    top, total, mixed, lane = joined_parts(own_ref, got_ref, heads)
    factor = float(HD) ** (-0.5)
    for h in range(heads):
        at = slice(h * HD, (h + 1) * HD)
        kv = slice(h // group * HD, (h // group + 1) * HD)
        query = query_ref[:, at].astype(jnp.float32)
        own = jnp.sum(query * key_ref[:, kv].astype(jnp.float32), axis=1, keepdims=True) * factor
        final = jnp.maximum(top[:, h : h + 1], own)
        old_scale = jnp.exp(top[:, h : h + 1] - final)
        own_weight = jnp.exp(own - final)
        whole = total[:, h : h + 1] * old_scale + own_weight
        part = mixed(h) * old_scale + own_weight * value_ref[:, kv].astype(jnp.float32)
        out_ref[:, at] = (part / whole).astype(out_ref.dtype)


def attention_kernel(
    lengths_ref, query_ref, keys_ref, values_ref, out_ref, keys, values, mixed, sems
):
    count, length, width = keys.shape
    heads = query_ref.shape[1]
    kv_heads = width // HD
    group = heads // kv_heads
    factor = float(HD) ** (-0.5)

    def copies(s):
        return (
            pltpu.make_async_copy(keys_ref.at[s], keys.at[s], sems.at[0, s]),
            pltpu.make_async_copy(values_ref.at[s], values.at[s], sems.at[1, s]),
        )

    for s in range(count):
        for copy in copies(s):
            copy.start()
    first = lax.axis_index("kvseq") * length
    places = first + lax.broadcasted_iota(jnp.int32, (heads, length), 1)
    lane = lax.broadcasted_iota(jnp.int32, (heads, 128), 1)
    top_columns = jnp.zeros((heads, 128), jnp.float32)
    total_columns = jnp.zeros((heads, 128), jnp.float32)
    for s in range(count):
        key_copy, value_copy = copies(s)
        key_copy.wait()
        query = query_ref[s].astype(jnp.bfloat16)
        scores = jnp.concatenate(
            [
                lax.dot_general(
                    query[j * group : (j + 1) * group],
                    keys[s, :, j * HD : (j + 1) * HD],
                    (((1,), (1,)), ((), ())),
                    preferred_element_type=jnp.float32,
                )
                for j in range(kv_heads)
            ],
            axis=0,
        )
        valid = places < lengths_ref[s]
        masked = jnp.where(valid, scores * factor, -1e30)
        high, low = high_low(jnp.max(masked, axis=1, keepdims=True))
        top = high + low
        weights = jnp.where(valid, jnp.exp(masked - top), 0.0)
        total = jnp.sum(weights, axis=1, keepdims=True)
        top_columns = jnp.where(lane == s, top, top_columns)
        total_columns = jnp.where(lane == s, total, total_columns)
        weights = weights.astype(jnp.bfloat16)
        value_copy.wait()
        for j in range(kv_heads):
            part = jnp.dot(
                weights[j * group : (j + 1) * group],
                values[s, :, j * HD : (j + 1) * HD],
                preferred_element_type=jnp.float32,
            )
            for g in range(group):
                mixed[j * group + g, s : s + 1, :] = part[g : g + 1]
    for h in range(heads):
        out_ref[:, h * HD : (h + 1) * HD] = mixed[h].astype(out_ref.dtype)

    def rows(columns):
        padded = jnp.concatenate([columns, jnp.zeros((128 - heads, 128), jnp.float32)], axis=0)
        return jnp.transpose(padded)[:count]

    lane = lax.broadcasted_iota(jnp.int32, (count, 128), 1)
    stats = packed_stats(rows(top_columns), rows(total_columns), lane, heads)
    out_ref[:, heads * HD :] = stats.astype(out_ref.dtype)


def pack_kernel(gate_ref, up_ref, residual_ref, sent_ref, kept_ref):
    half = gate_ref.shape[1] // 2
    upper = lax.axis_index("kvseq") & 1
    residual = residual_ref[...]
    squares = jnp.sum(residual * residual, axis=1, keepdims=True)
    high, low = high_low(squares)
    for ref, which in ((sent_ref, 1 - upper), (kept_ref, upper)):
        at = pl.ds(pl.multiple_of(which * half, 128), half)
        ref[:, :half] = gate_ref[:, at]
        ref[:, half : 2 * half] = up_ref[:, at]
        for i, part in enumerate((high, low)):
            start = 2 * half + i * 128
            ref[:, start : start + 128] = jnp.broadcast_to(part, (part.shape[0], 128)).astype(
                ref.dtype
            )


def order_kernel(mine_ref, other_ref, out_ref):
    half = mine_ref.shape[1]
    upper = lax.axis_index("kvseq") & 1
    out_ref[:, pl.ds(pl.multiple_of(upper * half, 128), half)] = mine_ref[...]
    out_ref[:, pl.ds(pl.multiple_of((1 - upper) * half, 128), half)] = other_ref[...]


def inner_kernel(own_ref, got_ref, out_ref):
    both, scalar = sums(own_ref, got_ref)
    scale = lax.rsqrt(scalar / D + epsilon)
    half = out_ref.shape[1]
    for at in range(0, half, 128):
        gate = both[:, at : at + 128] * scale
        upward = both[:, half + at : half + at + 128] * scale
        out_ref[:, at : at + 128] = (gate * jax.nn.sigmoid(gate) * upward).astype(out_ref.dtype)


def per_device(
    hidden,
    lengths,
    key_cache,
    value_cache,
    gain_in,
    w_query,
    w_key,
    w_value,
    w_output,
    gain_post,
    w_gate,
    w_up,
    w_down,
):
    stream = hidden.astype(jnp.float32)
    bits = bits_of("kvseq")
    seq_count = hidden.shape[0]
    q_width, k_width = w_query.shape[1], w_key.shape[1]
    query_heads, kv_heads = q_width // HD, k_width // HD
    per_group = query_heads // kv_heads
    position = lengths.astype(jnp.float32)
    frequency = rope_base ** (-jnp.arange(HD // 2, dtype=jnp.float32) * 2.0 / HD)
    angles = position[:, None] * frequency
    cosine, sine = jnp.cos(angles), jnp.sin(angles)
    turns = jnp.concatenate([cosine, cosine, -sine, sine], axis=1)
    squares = jnp.sum(stream * stream, axis=1)
    weighted = (stream * gain_in).astype(jnp.bfloat16)
    parts = [
        jnp.dot(weighted, w, preferred_element_type=jnp.float32).astype(jnp.bfloat16)
        for w in (w_query, w_key, w_value)
    ]
    scalars = [
        jnp.broadcast_to(a[:, None], (seq_count, 128)).astype(jnp.bfloat16)
        for a in split_high_low(squares)
    ]
    packed = jnp.concatenate(parts + scalars, axis=1)
    for bit in bits[:-1]:
        got = exchange(packed, "kvseq", bit)
        packed = local_call(sum_kernel, like(*packed.shape), packed, got, flops=WAIT_FLOPS)
    got = exchange(packed, "kvseq", bits[-1])
    query, new_keys, new_values, query_rows = local_call(
        query_kernel,
        [
            like(seq_count, q_width),
            like(seq_count, k_width),
            like(seq_count, k_width),
            like(seq_count, query_heads, HD, dtype=jnp.float32),
        ],
        packed,
        got,
        turns,
        flops=WAIT_FLOPS,
    )
    local_len = key_cache.shape[1]
    whole = pl.BlockSpec(memory_space=pltpu.VMEM)
    packed = pl.pallas_call(
        attention_kernel,
        out_shape=like(seq_count, q_width + 128),
        in_specs=[
            pl.BlockSpec(memory_space=pltpu.SMEM),
            whole,
            pl.BlockSpec(memory_space=pl.ANY),
            pl.BlockSpec(memory_space=pl.ANY),
        ],
        out_specs=whole,
        scratch_shapes=[
            pltpu.VMEM(key_cache.shape, key_cache.dtype),
            pltpu.VMEM(value_cache.shape, value_cache.dtype),
            pltpu.VMEM((query_heads, seq_count, HD), jnp.float32),
            pltpu.SemaphoreType.DMA((2, seq_count)),
        ],
        compiler_params=pltpu.CompilerParams(vmem_limit_bytes=8 << 20),
        cost_estimate=pl.CostEstimate(flops=WAIT_FLOPS, bytes_accessed=0, transcendentals=0),
        name="attention",
    )(lengths, query_rows, key_cache, value_cache)
    for bit in bits[:-1]:
        got = exchange(packed, "kvseq", bit)
        packed = local_call(join_kernel, like(*packed.shape), packed, got, flops=WAIT_FLOPS)
    got = exchange(packed, "kvseq", bits[-1])
    attended = local_call(
        attended_kernel,
        like(seq_count, query_heads * HD),
        packed,
        got,
        query,
        new_keys,
        new_values,
        flops=WAIT_FLOPS,
    )
    projected = jnp.dot(attended, w_output, preferred_element_type=jnp.float32)
    residual = stream + (projected + lax.ppermute(projected, "tensor", [(0, 1), (1, 0)]))
    weighted_post = (residual * gain_post).astype(jnp.bfloat16)
    gate_part = jnp.dot(weighted_post, w_gate, preferred_element_type=jnp.float32)
    upward_part = jnp.dot(weighted_post, w_up, preferred_element_type=jnp.float32)
    half = w_gate.shape[1] // 2
    sent, kept = local_call(
        pack_kernel,
        [like(seq_count, 2 * half + 256)] * 2,
        gate_part.astype(jnp.bfloat16),
        upward_part.astype(jnp.bfloat16),
        residual,
    )
    packed, target = kept, sent
    for step, bit in enumerate(bits):
        got = exchange(target, "kvseq", bit)
        if step + 1 < len(bits):
            packed = local_call(sum_kernel, like(*packed.shape), packed, got, flops=WAIT_FLOPS)
            target = packed
    mine = local_call(inner_kernel, like(seq_count, half), packed, got, flops=WAIT_FLOPS)
    other = exchange(mine, "kvseq", 1)
    inner = local_call(order_kernel, like(seq_count, 2 * half), mine, other)
    down_part = jnp.dot(inner, w_down, preferred_element_type=jnp.float32)
    down = down_part + lax.ppermute(down_part, "tensor", [(0, 1), (1, 0)])
    output = (residual + down).astype(jnp.bfloat16)
    return output, new_keys, new_values


def solution(mesh):
    placed = (
        P("groups", "kvseq"),
        P("groups"),
        P("groups", "kvseq", "tensor"),
        P("groups", "kvseq", "tensor"),
        P("kvseq"),
        P("kvseq", "tensor"),
        P("kvseq", "tensor"),
        P("kvseq", "tensor"),
        P("tensor", "kvseq"),
        P("kvseq"),
        P("kvseq", "tensor"),
        P("kvseq", "tensor"),
        P("tensor", "kvseq"),
    )
    return jax.shard_map(
        per_device,
        mesh=mesh,
        in_specs=placed,
        out_specs=(P("groups", "kvseq"), P("groups", "tensor"), P("groups", "tensor")),
        check_vma=False,
    )
```

```python
import functools

import jax
import jax.numpy as jnp
from jax import lax
from jax.experimental import pallas as pl
from jax.experimental.pallas import tpu as pltpu
from jax.sharding import PartitionSpec as P

D = 8192
HD = 128


epsilon = 1e-06
rope_base = 1000000.0


def high_low(x):
    high = x.astype(jnp.bfloat16).astype(jnp.float32)
    low = (x - high).astype(jnp.bfloat16).astype(jnp.float32)
    return high, low


def split_high_low(x):
    high = lax.reduce_precision(x, exponent_bits=8, mantissa_bits=7)
    return high, lax.reduce_precision(x - high, exponent_bits=8, mantissa_bits=7)


def exchange(x, axis, bit):
    count = lax.axis_size(axis)
    return lax.ppermute(x, axis, [(i, i ^ bit) for i in range(count)])


def bits_of(axis):
    count = lax.axis_size(axis)
    return [1 << i for i in range(count.bit_length() - 1)]


WAIT_FLOPS = 1500000000
FETCH_FLOPS = 1500000000


def local_call(kernel, outs, *args, flops=0, name=None):
    single = not isinstance(outs, (list, tuple))
    return pl.pallas_call(
        kernel,
        out_shape=outs,
        in_specs=[pl.BlockSpec(memory_space=pltpu.VMEM) for _ in args],
        out_specs=(
            pl.BlockSpec(memory_space=pltpu.VMEM)
            if single
            else [pl.BlockSpec(memory_space=pltpu.VMEM) for _ in outs]
        ),
        compiler_params=pltpu.CompilerParams(vmem_limit_bytes=4 << 20),
        cost_estimate=pl.CostEstimate(flops=flops, bytes_accessed=0, transcendentals=0),
        name=name,
    )(*args)


def like(*shape, dtype=jnp.bfloat16):
    return jax.ShapeDtypeStruct(shape, dtype)


def sums(own_ref, got_ref):
    width = own_ref.shape[1] - 256
    own = own_ref[...].astype(jnp.float32)
    both = own + got_ref[...].astype(jnp.float32)
    scalar = both[:, width : width + 128] + both[:, width + 128 :]
    return both[:, :width], scalar


def sum_kernel(own_ref, got_ref, out_ref):
    width = own_ref.shape[1] - 256
    both, scalar = sums(own_ref, got_ref)
    high, low = high_low(scalar)
    out_ref[:, :width] = both.astype(out_ref.dtype)
    out_ref[:, width : width + 128] = high.astype(out_ref.dtype)
    out_ref[:, width + 128 :] = low.astype(out_ref.dtype)


def project_kernel(hidden_ref, gain_ref, *refs, tile):
    weights = refs[:3]
    out_ref, held, sems = refs[3:]
    copies = []
    at = 0
    for w_ref in weights:
        for start in range(0, w_ref.shape[1], tile):
            copies.append(
                pltpu.make_async_copy(
                    w_ref.at[:, start : start + tile],
                    held.at[:, at : at + tile],
                    sems.at[len(copies)],
                )
            )
            at += tile
    for copy in copies:
        copy.start()
    stream = hidden_ref[...].astype(jnp.float32)
    weighted = (stream * gain_ref[...]).astype(jnp.bfloat16)
    squares = jnp.sum(stream * stream, axis=1, keepdims=True)
    for i, part in enumerate(high_low(squares)):
        out_ref[:, at + i * 128 : at + (i + 1) * 128] = jnp.broadcast_to(
            part, (part.shape[0], 128)
        ).astype(out_ref.dtype)
    for i, copy in enumerate(copies):
        copy.wait()
        here = slice(i * tile, (i + 1) * tile)
        out_ref[:, here] = jnp.dot(
            weighted, held[:, here], preferred_element_type=jnp.float32
        ).astype(out_ref.dtype)


def fetch_kernel(keys_ref, values_ref, keys, values, sems):
    copies = [
        pltpu.make_async_copy(keys_ref, keys, sems.at[0]),
        pltpu.make_async_copy(values_ref, values, sems.at[1]),
    ]
    for copy in copies:
        copy.start()
    for copy in copies:
        copy.wait()


def turned(x, cosine, sine):
    return x * cosine + pltpu.roll(x, HD // 2, 1) * sine


def query_kernel(own_ref, got_ref, angle_ref, query_ref, fresh_ref, rows_ref):
    both, scalar = sums(own_ref, got_ref)
    scale = lax.rsqrt(scalar / D + epsilon)
    cosine, sine = angle_ref[:, :HD], angle_ref[:, HD:]
    q_width, k_width = query_ref.shape[1], fresh_ref.shape[1] // 2
    for h in range(q_width // HD):
        part = both[:, h * HD : (h + 1) * HD] * scale
        part = turned(part, cosine, sine).astype(query_ref.dtype)
        query_ref[:, h * HD : (h + 1) * HD] = part
        count = part.shape[0]
        rows_ref[h * count : (h + 1) * count, :] = part.astype(rows_ref.dtype)
    for h in range(k_width // HD):
        at = q_width + h * HD
        part = both[:, at : at + HD] * scale
        fresh_ref[:, h * HD : (h + 1) * HD] = turned(part, cosine, sine).astype(fresh_ref.dtype)
        at = k_width + h * HD
        fresh_ref[:, at : at + HD] = (both[:, q_width + at : q_width + at + HD] * scale).astype(
            fresh_ref.dtype
        )


def shifted(x, lanes):
    size = x.shape[1]
    return pltpu.roll(x, lanes % size, 1)


def joined_scales(own_ref, got_ref, heads):
    width = heads * HD
    stats_own = own_ref[:, width:].astype(jnp.float32)
    stats_got = got_ref[:, width:].astype(jnp.float32)

    def tops(x):
        return x + shifted(x, -heads)

    def totals(x):
        return shifted(x, -2 * heads) + shifted(x, -3 * heads)

    top_own, top_got = tops(stats_own), tops(stats_got)
    top = jnp.maximum(top_own, top_got)
    lane = lax.broadcasted_iota(jnp.int32, top.shape, 1)
    used = lane < heads
    scale_own = jnp.exp(jnp.where(used, top_own - top, 0.0))
    scale_got = jnp.exp(jnp.where(used, top_got - top, 0.0))
    total = totals(stats_own) * scale_own + totals(stats_got) * scale_got

    return top, total, scale_own, scale_got, lane


def packed_stats(top, total, lane, heads):
    top_high, top_low = high_low(top)
    total_high, total_low = high_low(total)
    return jnp.where(
        lane < heads,
        top_high,
        jnp.where(
            lane < 2 * heads,
            shifted(top_low, heads),
            jnp.where(lane < 3 * heads, shifted(total_high, 2 * heads), shifted(total_low, 3 * heads)),
        ),
    )


def join_kernel(own_ref, got_ref, out_ref):
    heads = (own_ref.shape[1] - 128) // HD
    top, total, scale_own, scale_got, lane = joined_scales(own_ref, got_ref, heads)
    for h in range(heads):
        at = slice(h * HD, (h + 1) * HD)
        out_ref[:, at] = (
            own_ref[:, at].astype(jnp.float32) * scale_own[:, h : h + 1]
            + got_ref[:, at].astype(jnp.float32) * scale_got[:, h : h + 1]
        ).astype(out_ref.dtype)
    out_ref[:, heads * HD :] = packed_stats(top, total, lane, heads).astype(out_ref.dtype)


def own_kernel(query_ref, key_ref, out_ref):
    heads = query_ref.shape[1] // HD
    group = 2 * query_ref.shape[1] // key_ref.shape[1]
    lane = lax.broadcasted_iota(jnp.int32, out_ref.shape, 1)
    scores = jnp.zeros(out_ref.shape, jnp.float32)
    for h in range(heads):
        query = query_ref[:, h * HD : (h + 1) * HD].astype(jnp.float32)
        key = key_ref[:, h // group * HD : (h // group + 1) * HD].astype(jnp.float32)
        scores = jnp.where(lane == h, jnp.sum(query * key, axis=1, keepdims=True), scores)
    out_ref[...] = scores * float(HD) ** (-0.5)


def attended_kernel(own_ref, got_ref, score_ref, value_ref, out_ref):
    heads = out_ref.shape[1] // HD
    k_width = value_ref.shape[1] // 2
    group = out_ref.shape[1] // k_width
    top, total, scale_own, scale_got, lane = joined_scales(own_ref, got_ref, heads)
    used = lane < heads
    top = jnp.where(used, top, 0.0)
    total = jnp.where(used, total, 1.0)
    own = score_ref[...]
    final = jnp.maximum(top, own)
    old_scale = jnp.exp(top - final)
    own_weight = jnp.exp(own - final)
    inverse = 1.0 / (total * old_scale + own_weight)
    scale_own = scale_own * (old_scale * inverse)
    scale_got = scale_got * (old_scale * inverse)
    own_weight = own_weight * inverse
    for h in range(heads):
        at = slice(h * HD, (h + 1) * HD)
        kv = slice(k_width + h // group * HD, k_width + (h // group + 1) * HD)
        out_ref[:, at] = (
            own_ref[:, at].astype(jnp.float32) * scale_own[:, h : h + 1]
            + got_ref[:, at].astype(jnp.float32) * scale_got[:, h : h + 1]
            + value_ref[:, kv].astype(jnp.float32) * own_weight[:, h : h + 1]
        ).astype(out_ref.dtype)


def attention_kernel(lengths_ref, query_ref, keys, values, out_ref, scores, mixed):
    count, length, width = keys.shape
    heads = query_ref.shape[0] // count
    kv_heads = width // HD
    group = heads // kv_heads
    factor = float(HD) ** (-0.5)

    def rows(j, s):
        return pl.ds(j * group * count + s, group, stride=count)

    for s in range(count):
        for j in range(kv_heads):
            at = s * heads + j * group
            scores[at : at + group] = lax.dot_general(
                query_ref[rows(j, s), :].astype(jnp.bfloat16),
                keys[s, :, j * HD : (j + 1) * HD],
                (((1,), (1,)), ((), ())),
                preferred_element_type=jnp.float32,
            )
    first = lax.axis_index("kvseq") * length
    places = first + lax.broadcasted_iota(jnp.int32, (heads, length), 1)
    lane = lax.broadcasted_iota(jnp.int32, (heads, 128), 1)
    top_columns = jnp.zeros((heads, 128), jnp.float32)
    total_columns = jnp.zeros((heads, 128), jnp.float32)
    for s in range(count):
        valid = places < lengths_ref[s]
        masked = jnp.where(valid, scores[s * heads : (s + 1) * heads] * factor, -1e30)
        high, low = high_low(jnp.max(masked, axis=1, keepdims=True))
        top = high + low
        weights = jnp.where(valid, jnp.exp(masked - top), 0.0)
        total = jnp.sum(weights, axis=1, keepdims=True)
        top_columns = jnp.where(lane == s, top, top_columns)
        total_columns = jnp.where(lane == s, total, total_columns)
        scores[s * heads : (s + 1) * heads] = weights
    for s in range(count):
        for j in range(kv_heads):
            at = s * heads + j * group
            mixed[rows(j, s), :] = jnp.dot(
                scores[at : at + group].astype(jnp.bfloat16),
                values[s, :, j * HD : (j + 1) * HD],
                preferred_element_type=jnp.float32,
            )
    for h in range(heads):
        out_ref[:, h * HD : (h + 1) * HD] = mixed[h * count : (h + 1) * count].astype(out_ref.dtype)

    def stat_rows(columns):
        padded = jnp.concatenate([columns, jnp.zeros((128 - heads, 128), jnp.float32)], axis=0)
        return jnp.transpose(padded)[:count]

    lane = lax.broadcasted_iota(jnp.int32, (count, 128), 1)
    stats = packed_stats(stat_rows(top_columns), stat_rows(total_columns), lane, heads)
    out_ref[:, heads * HD :] = stats.astype(out_ref.dtype)


def pack_kernel(gate_ref, up_ref, residual_ref, sent_ref, kept_ref):
    half = gate_ref.shape[1] // 2
    upper = lax.axis_index("kvseq") & 1
    residual = residual_ref[...]
    squares = jnp.sum(residual * residual, axis=1, keepdims=True)
    high, low = high_low(squares)
    for ref, which in ((sent_ref, 1 - upper), (kept_ref, upper)):
        at = pl.ds(pl.multiple_of(which * half, 128), half)
        ref[:, :half] = gate_ref[:, at]
        ref[:, half : 2 * half] = up_ref[:, at]
        for i, part in enumerate((high, low)):
            start = 2 * half + i * 128
            ref[:, start : start + 128] = jnp.broadcast_to(part, (part.shape[0], 128)).astype(
                ref.dtype
            )


def order_kernel(mine_ref, other_ref, out_ref):
    half = mine_ref.shape[1]
    upper = lax.axis_index("kvseq") & 1
    out_ref[:, pl.ds(pl.multiple_of(upper * half, 128), half)] = mine_ref[...]
    out_ref[:, pl.ds(pl.multiple_of((1 - upper) * half, 128), half)] = other_ref[...]


def inner_kernel(own_ref, got_ref, out_ref):
    both, scalar = sums(own_ref, got_ref)
    scale = lax.rsqrt(scalar / D + epsilon)
    half = out_ref.shape[1]
    for at in range(0, half, 128):
        gate = both[:, at : at + 128] * scale
        upward = both[:, half + at : half + at + 128] * scale
        out_ref[:, at : at + 128] = (gate * jax.nn.sigmoid(gate) * upward).astype(out_ref.dtype)


def per_device(
    hidden,
    lengths,
    key_cache,
    value_cache,
    gain_in,
    w_query,
    w_key,
    w_value,
    w_output,
    gain_post,
    w_gate,
    w_up,
    w_down,
):
    stream = hidden.astype(jnp.float32)
    bits = bits_of("kvseq")
    seq_count = hidden.shape[0]
    q_width, k_width = w_query.shape[1], w_key.shape[1]
    query_heads, kv_heads = q_width // HD, k_width // HD
    per_group = query_heads // kv_heads
    position = lengths.astype(jnp.float32)
    frequency = rope_base ** (-jnp.arange(HD // 2, dtype=jnp.float32) * 2.0 / HD)
    angles = position[:, None] * frequency
    cosine, sine = jnp.cos(angles), jnp.sin(angles)
    turns = jnp.concatenate([cosine, cosine, -sine, sine], axis=1)
    in_vmem = pl.BlockSpec(memory_space=pltpu.VMEM)
    in_hbm = pl.BlockSpec(memory_space=pltpu.HBM)
    joined_width = q_width + 2 * k_width
    tile = k_width
    packed = pl.pallas_call(
        functools.partial(project_kernel, tile=tile),
        out_shape=like(seq_count, joined_width + 256),
        in_specs=[in_vmem, in_vmem, in_hbm, in_hbm, in_hbm],
        out_specs=in_vmem,
        scratch_shapes=[
            pltpu.VMEM((w_query.shape[0], joined_width), w_query.dtype),
            pltpu.SemaphoreType.DMA((joined_width // tile,)),
        ],
        compiler_params=pltpu.CompilerParams(vmem_limit_bytes=56 << 20),
        cost_estimate=pl.CostEstimate(flops=0, bytes_accessed=0, transcendentals=0),
        name="project",
    )(hidden, gain_in[None], w_query, w_key, w_value)
    keys, values = pl.pallas_call(
        fetch_kernel,
        out_shape=[like(*key_cache.shape), like(*value_cache.shape)],
        in_specs=[in_hbm, in_hbm],
        out_specs=[in_vmem, in_vmem],
        scratch_shapes=[pltpu.SemaphoreType.DMA((2,))],
        compiler_params=pltpu.CompilerParams(vmem_limit_bytes=1 << 20),
        cost_estimate=pl.CostEstimate(
            flops=FETCH_FLOPS, bytes_accessed=2 * key_cache.size, transcendentals=0
        ),
        name="fetch",
    )(key_cache, value_cache)
    for bit in bits[:-1]:
        got = exchange(packed, "kvseq", bit)
        packed = local_call(sum_kernel, like(*packed.shape), packed, got, flops=WAIT_FLOPS)
    got = exchange(packed, "kvseq", bits[-1])
    query, fresh, query_rows = local_call(
        query_kernel,
        [
            like(seq_count, q_width),
            like(seq_count, 2 * k_width),
            like(query_heads * seq_count, HD, dtype=jnp.float32),
        ],
        packed,
        got,
        turns,
        flops=WAIT_FLOPS,
    )
    packed = pl.pallas_call(
        attention_kernel,
        out_shape=like(seq_count, q_width + 128),
        in_specs=[pl.BlockSpec(memory_space=pltpu.SMEM), in_vmem, in_vmem, in_vmem],
        out_specs=in_vmem,
        scratch_shapes=[
            pltpu.VMEM((seq_count * query_heads, key_cache.shape[1]), jnp.float32),
            pltpu.VMEM((query_heads * seq_count, HD), jnp.float32),
        ],
        compiler_params=pltpu.CompilerParams(vmem_limit_bytes=4 << 20),
        cost_estimate=pl.CostEstimate(flops=WAIT_FLOPS, bytes_accessed=0, transcendentals=0),
        name="attention",
    )(lengths, query_rows, keys, values)
    own_scores = local_call(own_kernel, like(seq_count, 128, dtype=jnp.float32), query, fresh)
    for bit in bits[:-1]:
        got = exchange(packed, "kvseq", bit)
        packed = local_call(join_kernel, like(*packed.shape), packed, got, flops=WAIT_FLOPS)
    got = exchange(packed, "kvseq", bits[-1])
    attended = local_call(
        attended_kernel,
        like(seq_count, query_heads * HD),
        packed,
        got,
        own_scores,
        fresh,
        flops=WAIT_FLOPS,
    )
    projected = jnp.dot(attended, w_output, preferred_element_type=jnp.float32)
    residual = stream + (projected + lax.ppermute(projected, "tensor", [(0, 1), (1, 0)]))
    weighted_post = (residual * gain_post).astype(jnp.bfloat16)
    gate_part = jnp.dot(weighted_post, w_gate, preferred_element_type=jnp.float32)
    upward_part = jnp.dot(weighted_post, w_up, preferred_element_type=jnp.float32)
    half = w_gate.shape[1] // 2
    sent, kept = local_call(
        pack_kernel,
        [like(seq_count, 2 * half + 256)] * 2,
        gate_part.astype(jnp.bfloat16),
        upward_part.astype(jnp.bfloat16),
        residual,
    )
    packed, target = kept, sent
    for step, bit in enumerate(bits):
        got = exchange(target, "kvseq", bit)
        if step + 1 < len(bits):
            packed = local_call(sum_kernel, like(*packed.shape), packed, got, flops=WAIT_FLOPS)
            target = packed
    mine = local_call(inner_kernel, like(seq_count, half), packed, got, flops=WAIT_FLOPS)
    other = exchange(mine, "kvseq", 1)
    inner = local_call(order_kernel, like(seq_count, 2 * half), mine, other)
    down_part = jnp.dot(inner, w_down, preferred_element_type=jnp.float32)
    down = down_part + lax.ppermute(down_part, "tensor", [(0, 1), (1, 0)])
    output = (residual + down).astype(jnp.bfloat16)
    return output, fresh[:, :k_width], fresh[:, k_width:]


def solution(mesh):
    placed = (
        P("groups", "kvseq"),
        P("groups"),
        P("groups", "kvseq", "tensor"),
        P("groups", "kvseq", "tensor"),
        P("kvseq"),
        P("kvseq", "tensor"),
        P("kvseq", "tensor"),
        P("kvseq", "tensor"),
        P("tensor", "kvseq"),
        P("kvseq"),
        P("kvseq", "tensor"),
        P("kvseq", "tensor"),
        P("tensor", "kvseq"),
    )
    return jax.shard_map(
        per_device,
        mesh=mesh,
        in_specs=placed,
        out_specs=(P("groups", "kvseq"), P("groups", "tensor"), P("groups", "tensor")),
        check_vma=False,
    )
```
